256 devices in a mesh: space: 32 (over y, z_hi, core), band: 8 (over x, z_lo).
Axes of the slice: x: 4, y: 4, z: 8 (z_hi: 4, z_lo: 2; z = z_hi * 2 + z_lo), core: 2. Of those that a mesh axis runs over, the one named last changes fastest.
Arguments:
- orbitals: float32 [320, 128, 512], P('band', 'space'), may hold values from -6 to 6
- potential: float32 [128, 512], P('space'), may hold values from -2 to 0
- rotation: float32 [320, 320], replicated, may hold values from -0.3125 to 0.3125
Outputs:
- rotated: float32 [320, 128, 512], P('band', 'space')
The draws below stay inside these ranges and needn't reach their ends.
All inputs are finite; a program needn't handle non-finite values.
Results may differ from the reference program's by a relative error of at most 0.00007.
Values sent between devices are 32-bit elements; how exact they have to be, the bound alone decides.
No kernel may reach another device: no remote copies, remote signals or barrier semaphores. Data moves between devices by JAX's collectives and lax.ppermute only.
A program may use at most 64 MiB of HBM per device.

```python
import jax
import jax.numpy as jnp
from jax import lax

NORB = 320
DEG = 4
NY = 16
NZ = 32
PLANE = 512
NX = 128


def block_levels(stream_key, extent, split, least, largest):
    level, own = 1.0, jax.random.fold_in(stream_key, 6)
    for axis_at, blocks in split:
        draws = jnp.exp(jax.random.uniform(jax.random.fold_in(own, axis_at), (blocks,), jnp.float32, least / len(split), largest / len(split)))
        level = level * jnp.repeat(draws, extent[axis_at] // blocks).reshape([-1 if axis == axis_at else 1 for axis in range(len(extent))])
    return level


def scatter_about(key, extent, width, reach, shards=(), held_as=jnp.bfloat16):
    entries = width * jax.random.normal(key, extent, jnp.float32)
    if shards:
        entries = entries * block_levels(key, extent, shards, -0.22, 0.18)
    return jnp.clip(entries, -reach, reach).astype(held_as)


def setup_inputs(seed: int = 0) -> dict:
    arg_keys = jax.random.split(jax.random.key(seed), 4)
    return {
        "orbitals": scatter_about(arg_keys[0], (NORB, NX, PLANE), 1.0, 6.0, ((0, 8), (1, 32)), jnp.float32),
        "potential": jnp.clip(-2.0 + 2.0 * jax.random.uniform(arg_keys[1], (NX, PLANE), jnp.float32) ** block_levels(arg_keys[1], (NX, PLANE), ((0, 32),), -0.2, 0.2), -2.0, 0.0),
        "rotation": scatter_about(arg_keys[2], (NORB, NORB), NORB ** -0.5, 0.3125, (), jnp.float32),
    }


coef_lap = (-205.0 / 72.0, 8.0 / 5.0, -1.0 / 5.0, 8.0 / 315.0, -1.0 / 560.0)
center_val = 6.0
half_width = 4.0


def hamil(field, pot_grid):
    lap = (3.0 * coef_lap[0]) * field
    for shift_k in range(1, 5):
        for axis_num in (1, 2, 3):
            lap = lap + coef_lap[shift_k] * (jnp.roll(field, shift_k, axis_num) + jnp.roll(field, -shift_k, axis_num))
    return -0.5 * lap + pot_grid[None] * field


def filter_block(block, pot_grid):
    prev_y = block
    curr_y = (hamil(block, pot_grid) - center_val * block) / half_width
    for step in range(1, DEG):
        next_y = 2.0 * (hamil(curr_y, pot_grid) - center_val * curr_y) / half_width - prev_y
        prev_y = curr_y
        curr_y = next_y
    return curr_y


def reference(orbitals, potential, rotation):
    pot_grid = potential.reshape(NX, NY, NZ)
    blocks = orbitals.reshape(NORB // 16, 16, NX, NY, NZ)
    filtered = lax.map(lambda blk: filter_block(blk, pot_grid), blocks)
    filtered = filtered.reshape(NORB, NX * PLANE)
    rotated = lax.dot_general(rotation, filtered, (((0,), (0,)), ((), ())), precision=lax.Precision.HIGHEST, preferred_element_type=jnp.float32)
    return rotated.reshape(NORB, NX, PLANE)
```

```python
import jax
import jax.numpy as jnp
import numpy as np
from jax import lax
from jax.experimental import pallas as pl
from jax.experimental.pallas import tpu as pltpu
from jax.sharding import Mesh
from jax.sharding import PartitionSpec as P

DEG = 4
NY = 16
NZ = 32
PLANE = NY * NZ
NORB = 320
BAND = ("x", "zl")
SPACE = ("y", "zh", "core")

coef_lap = (-205.0 / 72.0, 8.0 / 5.0, -1.0 / 5.0, 8.0 / 315.0, -1.0 / 560.0)
center_val = 6.0
half_width = 4.0
SCALE = -0.5 / half_width


def lateral():
    def ring(n):
        m = np.zeros((n, n))
        for k in range(1, 5):
            for i in range(n):
                m[i, (i + k) % n] += coef_lap[k]
                m[i, (i - k) % n] += coef_lap[k]
        return m

    lap = np.kron(np.eye(NY), ring(NZ)) + np.kron(ring(NY), np.eye(NZ))
    lap += 3.0 * coef_lap[0] * np.eye(PLANE)
    full = (SCALE * lap - (center_val / half_width) * np.eye(PLANE)).astype(np.float32)
    high = full.astype(jnp.bfloat16)
    low = (full - high.astype(np.float32)).astype(jnp.bfloat16)
    return high, low


def split(v):
    high = v.astype(jnp.bfloat16)
    low = (v - high.astype(jnp.float32)).astype(jnp.bfloat16)
    return high, low


def filter_kernel(mine_ref, low_ref, high_ref, mh_ref, ml_ref, out_ref, pot_ref, *bufs):
    core = lax.axis_index("core")
    at = 0
    for ref in (low_ref, mine_ref, high_ref):
        for zh in range(ref.shape[0]):
            for s in range(2):
                for q in range(6):
                    for j in range(4):
                        piece = ref[zh, s, q, :, j * 128 : (j + 1) * 128]
                        if q < 5:
                            bufs[0][q, j, at : at + 4, :] = piece
                        else:
                            pot_ref[j, at : at + 4, :] = piece * (1.0 / half_width)
                at += 4
    for step in range(1, DEG + 1):
        rows = 64 - 8 * step
        cur, nxt = bufs[step - 1], bufs[step]
        lanes = [cur[:, j, 4 : 4 + rows, :].reshape(5 * rows, 128) for j in range(4)]
        field = jnp.concatenate(lanes, axis=1)
        high, low = split(field)
        dot = lambda a, b: jnp.dot(a, b, preferred_element_type=jnp.float32)
        lat = dot(high, mh_ref[...]) + (dot(low, mh_ref[...]) + dot(high, ml_ref[...]))
        for q in range(5):
            for j in range(4):
                acc = lat[q * rows : (q + 1) * rows, j * 128 : (j + 1) * 128]
                center = cur[q, j, 4 : 4 + rows, :]
                acc = acc + pot_ref[j, 4 * step : 4 * step + rows, :] * center
                for k in range(1, 5):
                    acc = acc + (SCALE * coef_lap[k]) * (
                        cur[q, j, 4 + k : 4 + k + rows, :] + cur[q, j, 4 - k : 4 - k + rows, :]
                    )
                if step > 1:
                    acc = 2.0 * acc - bufs[step - 2][q, j, 8 : 8 + rows, :]
                if step < DEG:
                    nxt[q, j, 0:rows, :] = acc
                else:
                    half, tile = divmod(j, 2)
                    for zh in range(4):
                        for s in range(2):
                            row = (half * 4 + zh) * 10 + q * 2 + tile
                            at = zh * 8 + s * 4
                            out_ref[s ^ core, pl.ds(row, 4, stride=80), :] = acc[at : at + 4, :]


def run_filter(mine, low, high):
    mh, ml = lateral()
    vmem = pl.BlockSpec(memory_space=pltpu.VMEM)
    return pl.pallas_call(
        filter_kernel,
        out_shape=jax.ShapeDtypeStruct((2, 320, 128), jnp.float32),
        in_specs=[vmem] * 5,
        out_specs=vmem,
        scratch_shapes=[pltpu.VMEM((4, 64, 128), jnp.float32)]
        + [pltpu.VMEM((5, 4, 64 - 8 * s, 128), jnp.float32) for s in range(DEG)]
        + [pltpu.VMEM((8, 128), jnp.float32)],
        compiler_params=pltpu.CompilerParams(vmem_limit_bytes=24 << 20),
        name="filter",
    )(mine, low, high, jnp.asarray(mh), jnp.asarray(ml))


def rotate_kernel(weights_ref, field_ref, out_ref):
    field = jnp.concatenate(
        [field_ref[pl.ds(tile, NORB, stride=2), :] for tile in range(2)], axis=1
    )
    out_ref[...] = jnp.dot(
        weights_ref[...],
        field,
        precision=lax.Precision.HIGHEST,
        preferred_element_type=jnp.float32,
    )


def run_rotate(weights, field):
    vmem = pl.BlockSpec(memory_space=pltpu.VMEM)
    return pl.pallas_call(
        rotate_kernel,
        out_shape=jax.ShapeDtypeStruct((NORB, 256), jnp.float32),
        in_specs=[vmem] * 2,
        out_specs=vmem,
        compiler_params=pltpu.CompilerParams(vmem_limit_bytes=8 << 20),
        name="rotate",
    )(weights, field)


SWAP = [(0, 1), (1, 0)]
UP = [(0, 1), (1, 2), (2, 3), (3, 0)]
DOWN = [(1, 0), (2, 1), (3, 2), (0, 3)]


def local(orbitals, potential, rotation):
    core = lax.axis_index("core")
    pairs = orbitals.reshape(20, 2, 4, PLANE)
    give = lax.dynamic_index_in_dim(pairs, 1 - core, 1, keepdims=False)
    keep = lax.dynamic_index_in_dim(pairs, core, 1, keepdims=False)
    give = jnp.concatenate([give, potential[None]], axis=0)
    got = lax.ppermute(give, "core", SWAP)

    def six(block, pot):
        block = block.reshape(4, 5, 4, PLANE)
        return jnp.concatenate(
            [block, jnp.broadcast_to(pot[None, None], (4, 1, 4, PLANE))], axis=1
        )

    own = six(keep, potential)
    other = six(got[:20], got[20])
    payload = jnp.where(
        core == 0,
        jnp.stack([own, other], axis=1),
        jnp.stack([other, own], axis=1),
    )
    mine = lax.all_to_all(payload, "zh", 0, 0, tiled=True)
    low = lax.ppermute(mine[2:4], "y", UP)
    high = lax.ppermute(mine[0:2], "y", DOWN)
    halves = run_filter(mine, low, high)
    got = lax.ppermute(halves[1], "core", SWAP)
    own = halves[0].reshape(32, 5, 1, 2, 128)
    other = got.reshape(32, 5, 1, 2, 128)
    payload = jnp.where(
        core == 0,
        jnp.concatenate([own, other], axis=2),
        jnp.concatenate([other, own], axis=2),
    )
    columns = lax.all_to_all(payload.reshape(32, 5, 4, 128), BAND + ("zh",), 0, 0, tiled=True)
    turned = run_rotate(rotation.T, columns.reshape(640, 128))
    back = lax.all_to_all(turned.reshape(8, 40, 256), BAND, 0, 0, tiled=True)
    return back.reshape(4, 2, 40, 256).transpose(2, 0, 1, 3).reshape(40, 4, PLANE)


def solution(mesh):
    fine = Mesh(mesh.devices.reshape(4, 4, 2, 4, 2), SPACE + BAND)
    placed = (P(BAND, SPACE, None), P(SPACE, None), P())
    return jax.shard_map(
        local, mesh=fine, in_specs=placed, out_specs=P(BAND, SPACE, None), check_vma=False
    )
```

```python
import jax
import jax.numpy as jnp
import numpy as np
from jax import lax
from jax.experimental import pallas as pl
from jax.experimental.pallas import tpu as pltpu
from jax.sharding import Mesh
from jax.sharding import PartitionSpec as P

DEG = 4
NY = 16
NZ = 32
PLANE = NY * NZ
NORB = 320
BAND = ("x", "zl")
SPACE = ("y", "zh", "core")

coef_lap = (-205.0 / 72.0, 8.0 / 5.0, -1.0 / 5.0, 8.0 / 315.0, -1.0 / 560.0)
center_val = 6.0
half_width = 4.0
SCALE = -0.5 / half_width


def lateral():
    def ring(n):
        m = np.zeros((n, n))
        for k in range(1, 5):
            for i in range(n):
                m[i, (i + k) % n] += coef_lap[k]
                m[i, (i - k) % n] += coef_lap[k]
        return m

    lap = np.kron(np.eye(NY), ring(NZ)) + np.kron(ring(NY), np.eye(NZ))
    lap += 3.0 * coef_lap[0] * np.eye(PLANE)
    full = (SCALE * lap - (center_val / half_width) * np.eye(PLANE)).astype(np.float32)
    high = full.astype(jnp.bfloat16)
    low = (full - high.astype(np.float32)).astype(jnp.bfloat16)
    return high, low


def split(v):
    high = v.astype(jnp.bfloat16)
    low = (v - high.astype(jnp.float32)).astype(jnp.bfloat16)
    return high, low


def filter_kernel(*refs):
    pieces, halos = refs[0:4], refs[4:8]
    mh_ref, ml_ref, out_ref, pot_ref = refs[8:12]
    bufs = refs[12:]
    core, zh_here = lax.axis_index("core"), lax.axis_index("zh")
    for ahead in range(4):
        zh = lax.rem(zh_here + (4 - ahead), 4)
        inside = 16 + zh * 8
        outside = jnp.where(zh >= 2, (zh - 2) * 8, 48 + zh * 8)
        for ref, at in ((pieces[ahead], inside), (halos[ahead], outside)):
            rows = pl.ds(pl.multiple_of(at, 8), 8)
            for q in range(6):
                for j in range(4):
                    part = jnp.concatenate(
                        [ref[s, q, :, j * 128 : (j + 1) * 128] for s in range(2)], axis=0
                    )
                    if q < 5:
                        bufs[0][q, j, rows, :] = part
                    else:
                        pot_ref[j, rows, :] = part * (1.0 / half_width)
    for step in range(1, DEG + 1):
        rows = 64 - 8 * step
        cur, nxt = bufs[step - 1], bufs[step % DEG]
        lanes = [cur[:, j, 4 : 4 + rows, :].reshape(5 * rows, 128) for j in range(4)]
        field = jnp.concatenate(lanes, axis=1)
        high, low = split(field)
        dot = lambda a, b: jnp.dot(a, b, preferred_element_type=jnp.float32)
        lat = dot(high, mh_ref[...]) + (dot(low, mh_ref[...]) + dot(high, ml_ref[...]))
        for q in range(5):
            for j in range(4):
                acc = lat[q * rows : (q + 1) * rows, j * 128 : (j + 1) * 128]
                center = cur[q, j, 4 : 4 + rows, :]
                acc = acc + pot_ref[j, 4 * step : 4 * step + rows, :] * center
                for k in range(1, 5):
                    acc = acc + (SCALE * coef_lap[k]) * (
                        cur[q, j, 4 + k : 4 + k + rows, :] + cur[q, j, 4 - k : 4 - k + rows, :]
                    )
                if step > 1:
                    acc = 2.0 * acc - bufs[step - 2][q, j, 8 : 8 + rows, :]
                if step < DEG:
                    nxt[q, j, 0:rows, :] = acc
                    continue
                half, tile = divmod(j, 2)
                for zh in range(4):
                    for s in range(2):
                        row = (half * 4 + zh) * 10 + q * 2 + tile
                        at = zh * 8 + s * 4
                        out_ref[s ^ core, pl.ds(row, 4, stride=80), :] = acc[at : at + 4, :]


def run_filter(pieces, halos):
    mh, ml = lateral()
    vmem = pl.BlockSpec(memory_space=pltpu.VMEM)
    return pl.pallas_call(
        filter_kernel,
        out_shape=jax.ShapeDtypeStruct((2, 320, 128), jnp.float32),
        in_specs=[vmem] * 10,
        out_specs=vmem,
        scratch_shapes=[pltpu.VMEM((4, 64, 128), jnp.float32)]
        + [pltpu.VMEM((5, 4, 64 - 8 * s, 128), jnp.float32) for s in range(DEG)],
        compiler_params=pltpu.CompilerParams(vmem_limit_bytes=24 << 20),
        name="filter",
    )(*pieces, *halos, jnp.asarray(mh), jnp.asarray(ml))


def merge_kernel(kept_ref, got_ref, out_ref):
    core = lax.axis_index("core")
    for side in range(2):

        @pl.when(core == side)
        def _():
            for tile in range(2):
                for slot, ref in ((side, kept_ref), (1 - side, got_ref)):
                    out_ref[pl.ds(slot * 2 + tile, 160, stride=4), :] = ref[
                        pl.ds(tile, 160, stride=2), :
                    ]


def run_merge(kept, got):
    vmem = pl.BlockSpec(memory_space=pltpu.VMEM)
    return pl.pallas_call(
        merge_kernel,
        out_shape=jax.ShapeDtypeStruct((640, 128), jnp.float32),
        in_specs=[vmem] * 2,
        out_specs=vmem,
        compiler_params=pltpu.CompilerParams(vmem_limit_bytes=4 << 20),
        name="merge",
    )(kept, got)


def turn_kernel(weights_ref, high_ref, low_ref):
    high_ref[...], low_ref[...] = split(weights_ref[...].T)


def run_turn(rotation):
    vmem = pl.BlockSpec(memory_space=pltpu.VMEM)
    return pl.pallas_call(
        turn_kernel,
        out_shape=[jax.ShapeDtypeStruct((NORB, NORB), jnp.bfloat16)] * 2,
        in_specs=[vmem],
        out_specs=[vmem] * 2,
        compiler_params=pltpu.CompilerParams(vmem_limit_bytes=8 << 20),
        name="turn",
    )(rotation)


def rotate_kernel(wh_ref, wl_ref, field_ref, out_ref):
    field = jnp.concatenate(
        [field_ref[pl.ds(tile, NORB, stride=2), :] for tile in range(2)], axis=1
    )
    high, low = split(field)
    dot = lambda a, b: jnp.dot(a, b, preferred_element_type=jnp.float32)
    wh = wh_ref[...]
    out_ref[...] = dot(wh, high) + (dot(wh, low) + dot(wl_ref[...], high))


def run_rotate(weights, field):
    vmem = pl.BlockSpec(memory_space=pltpu.VMEM)
    return pl.pallas_call(
        rotate_kernel,
        out_shape=jax.ShapeDtypeStruct((NORB, 256), jnp.float32),
        in_specs=[vmem] * 3,
        out_specs=vmem,
        compiler_params=pltpu.CompilerParams(vmem_limit_bytes=8 << 20),
        name="rotate",
    )(*weights, field)


SWAP = [(0, 1), (1, 0)]


def ahead_by(step):
    return [(zh, (zh + step) % 4) for zh in range(4)]


def outward(ahead):
    pairs = []
    for y in range(4):
        for zh in range(4):
            way = 1 if (zh - ahead) % 4 >= 2 else -1
            pairs.append((y * 4 + zh, (y + way) % 4 * 4 + zh))
    return pairs


def local(orbitals, potential, rotation):
    core, zh_here = lax.axis_index("core"), lax.axis_index("zh")
    pairs = orbitals.reshape(20, 2, 4, PLANE)
    give = lax.dynamic_index_in_dim(pairs, 1 - core, 1, keepdims=False)
    keep = lax.dynamic_index_in_dim(pairs, core, 1, keepdims=False)
    give = jnp.concatenate([give, potential[None]], axis=0)
    got = lax.ppermute(give, "core", SWAP)

    def six(block, pot):
        block = block.reshape(4, 5, 4, PLANE)
        return jnp.concatenate(
            [block, jnp.broadcast_to(pot[None, None], (4, 1, 4, PLANE))], axis=1
        )

    own = six(keep, potential)
    other = six(got[:20], got[20])
    payload = jnp.where(
        core == 0,
        jnp.stack([own, other], axis=1),
        jnp.stack([other, own], axis=1),
    )
    pieces, halos = [None] * 4, [None] * 4
    for ahead in (2, 1, 3, 0):
        piece = lax.dynamic_index_in_dim(payload, (zh_here + ahead) % 4, 0, keepdims=False)
        pieces[ahead] = lax.ppermute(piece, "zh", ahead_by(ahead)) if ahead else piece
    for ahead in (0, 2, 1, 3):
        halos[ahead] = lax.ppermute(pieces[ahead], ("y", "zh"), outward(ahead))
    halves = run_filter(pieces, halos)
    got = lax.ppermute(halves[1], "core", SWAP)
    weights = run_turn(rotation)
    got, weights = lax.optimization_barrier((got, weights))
    merged = run_merge(halves[0], got)
    columns = lax.all_to_all(merged.reshape(32, 5, 4, 128), BAND + ("zh",), 0, 0, tiled=True)
    turned = run_rotate(weights, columns.reshape(640, 128))
    back = lax.all_to_all(turned.reshape(8, 40, 256), BAND, 0, 0, tiled=True)
    return back.reshape(4, 2, 40, 256).transpose(2, 0, 1, 3).reshape(40, 4, PLANE)


def solution(mesh):
    fine = Mesh(mesh.devices.reshape(4, 4, 2, 4, 2), SPACE + BAND)
    placed = (P(BAND, SPACE, None), P(SPACE, None), P())
    return jax.shard_map(
        local, mesh=fine, in_specs=placed, out_specs=P(BAND, SPACE, None), check_vma=False
    )
```

```python
import jax
import jax.numpy as jnp
import numpy as np
from jax import lax
from jax.experimental import pallas as pl
from jax.experimental.pallas import tpu as pltpu
from jax.sharding import Mesh
from jax.sharding import PartitionSpec as P


DEG = 4
NY = 16
NZ = 32
PLANE = NY * NZ
NORB = 320
BAND = ("x", "zl")
SPACE = ("y", "zh", "core")

coef_lap = (-205.0 / 72.0, 8.0 / 5.0, -1.0 / 5.0, 8.0 / 315.0, -1.0 / 560.0)
center_val = 6.0
half_width = 4.0
SCALE = -0.5 / half_width


def lateral():
    def ring(n):
        m = np.zeros((n, n))
        for k in range(1, 5):
            for i in range(n):
                m[i, (i + k) % n] += coef_lap[k]
                m[i, (i - k) % n] += coef_lap[k]
        return m

    lap = np.kron(np.eye(NY), ring(NZ)) + np.kron(ring(NY), np.eye(NZ))
    lap += 3.0 * coef_lap[0] * np.eye(PLANE)
    full = (SCALE * lap - (center_val / half_width) * np.eye(PLANE)).astype(np.float32)
    high = full.astype(jnp.bfloat16)
    low = (full - high.astype(np.float32)).astype(jnp.bfloat16)
    return high, low


def split(v):
    high = v.astype(jnp.bfloat16)
    low = (v - high.astype(jnp.float32)).astype(jnp.bfloat16)
    return high, low


def place(ref, at, buf_ref, pot_ref):
    rows = pl.ds(pl.multiple_of(at, 8), 8)
    for q in range(6):
        for j in range(4):
            part = jnp.concatenate(
                [ref[s, q, :, j * 128 : (j + 1) * 128] for s in range(2)], axis=0
            )
            if q < 5:
                buf_ref[q, j, rows, :] = part
            else:
                pot_ref[j, rows, :] = part * (1.0 / half_width)


def advance(spans, cur, prev, pot_ref, pot_at, mh_ref, ml_ref, emit):
    tall = sum(count for _, count in spans) * 5
    lanes = []
    for j in range(4):
        parts = [cur[q, j, 4 + at : 4 + at + n, :] for q in range(5) for at, n in spans]
        lanes.append(jnp.concatenate(parts, axis=0))
    high, low = split(jnp.concatenate(lanes, axis=1))
    dot = lambda a, b: jnp.dot(a, b, preferred_element_type=jnp.float32)
    lat = dot(high, mh_ref[...]) + (dot(low, mh_ref[...]) + dot(high, ml_ref[...]))
    row = 0
    for q in range(5):
        for at, n in spans:
            for j in range(4):
                acc = lat[row : row + n, j * 128 : (j + 1) * 128]
                acc = acc + pot_ref[j, pot_at + at : pot_at + at + n, :] * lanes[j][row : row + n]
                for k in range(1, 5):
                    acc = acc + (SCALE * coef_lap[k]) * (
                        cur[q, j, 4 + at + k : 4 + at + k + n, :]
                        + cur[q, j, 4 + at - k : 4 + at - k + n, :]
                    )
                if prev is not None:
                    acc = 2.0 * acc - prev[q, j, 8 + at : 8 + at + n, :]
                emit(q, j, at, n, acc)
            row += n
    assert row == tall


def saver(ref):
    def emit(q, j, at, n, acc):
        ref[q, j, at : at + n, :] = acc

    return emit


def inner_kernel(*refs):
    mh_ref, ml_ref, pot_ref = refs[4:7]
    levels = refs[7:11]
    zh_here = lax.axis_index("zh")
    for ahead in range(4):
        place(refs[ahead], lax.rem(zh_here + (4 - ahead), 4) * 8, levels[0], pot_ref)
    for step in range(1, DEG):
        prev = levels[step - 2] if step > 1 else None
        spans = ((0, 32 - 8 * step),)
        advance(
            spans, levels[step - 1], prev, pot_ref, 4 * step, mh_ref, ml_ref, saver(levels[step])
        )


def outer_kernel(*refs):
    halos, mh_ref, ml_ref, own_pot = refs[0:4], *refs[4:7]
    inner, out_ref, pot_ref = refs[7:11], refs[11], refs[12]
    levels = refs[13:17]
    zh_here = lax.axis_index("zh")
    for ahead in range(4):
        zh = lax.rem(zh_here + (4 - ahead), 4)
        place(halos[ahead], jnp.where(zh >= 2, (zh - 2) * 8, 48 + zh * 8), levels[0], pot_ref)
    pot_ref[:, 16:48, :] = own_pot[...]
    for step in range(DEG):
        levels[step][:, :, 16 : 48 - 8 * step, :] = inner[step][...]

    def emit(q, j, at, n, acc):
        half, tile = divmod(j, 2)
        for plane in range(at, at + n, 4):
            zh, s = divmod(plane // 4, 2)
            row = ((half * 4 + zh) * 2 + s) * 10 + q * 2 + tile
            out_ref[pl.ds(row, 4, stride=160), :] = acc[plane - at : plane - at + 4, :]

    for step in range(1, DEG + 1):
        prev = levels[step - 2] if step > 1 else None
        spans = ((0, 16), (48 - 8 * step, 16))
        advance(
            spans,
            levels[step - 1],
            prev,
            pot_ref,
            4 * step,
            mh_ref,
            ml_ref,
            emit if step == DEG else saver(levels[step]),
        )


def stack_of(rows):
    return (5, 4, rows, 128)


def run_inner(pieces, lat):
    vmem = pl.BlockSpec(memory_space=pltpu.VMEM)
    shapes = [(4, 32, 128)] + [stack_of(32 - 8 * s) for s in range(DEG)]
    return pl.pallas_call(
        inner_kernel,
        out_shape=[jax.ShapeDtypeStruct(shape, jnp.float32) for shape in shapes],
        in_specs=[vmem] * 6,
        out_specs=[vmem] * 5,
        compiler_params=pltpu.CompilerParams(vmem_limit_bytes=16 << 20),
        cost_estimate=pl.CostEstimate(flops=2 << 30, bytes_accessed=4 << 20, transcendentals=0),
        name="inner",
    )(*pieces, *lat)


def run_outer(halos, lat, found):
    vmem = pl.BlockSpec(memory_space=pltpu.VMEM)
    return pl.pallas_call(
        outer_kernel,
        out_shape=jax.ShapeDtypeStruct((640, 128), jnp.float32),
        in_specs=[vmem] * 11,
        out_specs=vmem,
        scratch_shapes=[pltpu.VMEM((4, 64, 128), jnp.float32)]
        + [pltpu.VMEM(stack_of(64 - 8 * s), jnp.float32) for s in range(DEG)],
        compiler_params=pltpu.CompilerParams(vmem_limit_bytes=20 << 20),
        name="outer",
    )(*halos, *lat, *found)


def turn_kernel(weights_ref, high_ref, low_ref):
    high_ref[...], low_ref[...] = split(weights_ref[...].T)


def run_turn(rotation):
    vmem = pl.BlockSpec(memory_space=pltpu.VMEM)
    return pl.pallas_call(
        turn_kernel,
        out_shape=[jax.ShapeDtypeStruct((NORB, NORB), jnp.bfloat16)] * 2,
        in_specs=[vmem],
        out_specs=[vmem] * 2,
        compiler_params=pltpu.CompilerParams(vmem_limit_bytes=8 << 20),
        name="turn",
    )(rotation)


def rotate_kernel(wh_ref, wl_ref, field_ref, out_ref):
    field = jnp.concatenate(
        [field_ref[pl.ds(tile, NORB, stride=2), :] for tile in range(2)], axis=1
    )
    high, low = split(field)
    dot = lambda a, b: jnp.dot(a, b, preferred_element_type=jnp.float32)
    wh = wh_ref[...]
    out_ref[...] = dot(wh, high) + (dot(wh, low) + dot(wl_ref[...], high))


def run_rotate(weights, field):
    vmem = pl.BlockSpec(memory_space=pltpu.VMEM)
    return pl.pallas_call(
        rotate_kernel,
        out_shape=jax.ShapeDtypeStruct((NORB, 256), jnp.float32),
        in_specs=[vmem] * 3,
        out_specs=vmem,
        compiler_params=pltpu.CompilerParams(vmem_limit_bytes=8 << 20),
        name="rotate",
    )(*weights, field)


SWAP = [(0, 1), (1, 0)]


def ahead_by(step):
    return [(zh, (zh + step) % 4) for zh in range(4)]


def outward(ahead):
    pairs = []
    for y in range(4):
        for zh in range(4):
            way = 1 if (zh - ahead) % 4 >= 2 else -1
            pairs.append((y * 4 + zh, (y + way) % 4 * 4 + zh))
    return pairs


def local(orbitals, potential, rotation):
    core, zh_here = lax.axis_index("core"), lax.axis_index("zh")
    pairs = orbitals.reshape(4, 2, 5, 4, PLANE)
    give = lax.dynamic_index_in_dim(pairs, 1 - core, 1, keepdims=False).reshape(20, 4, PLANE)
    keep = lax.dynamic_index_in_dim(pairs, core, 1, keepdims=False)
    give = jnp.concatenate([give, potential[None]], axis=0)
    got = lax.ppermute(give, "core", SWAP)

    def six(block, pot):
        block = block.reshape(4, 5, 4, PLANE)
        return jnp.concatenate(
            [block, jnp.broadcast_to(pot[None, None], (4, 1, 4, PLANE))], axis=1
        )

    own = six(keep, potential)
    other = six(got[:20], got[20])
    payload = jnp.where(
        core == 0,
        jnp.stack([own, other], axis=1),
        jnp.stack([other, own], axis=1),
    )
    pieces, halos = [None] * 4, [None] * 4
    for ahead in (2, 1, 3, 0):
        piece = lax.dynamic_index_in_dim(payload, (zh_here + ahead) % 4, 0, keepdims=False)
        pieces[ahead] = lax.ppermute(piece, "zh", ahead_by(ahead)) if ahead else piece
    for ahead in (0, 2, 1, 3):
        halos[ahead] = lax.ppermute(pieces[ahead], ("y", "zh"), outward(ahead))
    lat = tuple(jnp.asarray(part) for part in lateral())
    found = run_inner(pieces, lat)
    filtered = run_outer(halos, lat, found)
    weights = run_turn(rotation)
    filtered, weights = lax.optimization_barrier((filtered, weights))
    columns = lax.all_to_all(
        filtered.reshape(64, 5, 2, 128), BAND + ("zh", "core"), 0, 0, tiled=True
    )
    turned = run_rotate(weights, columns.reshape(640, 128))
    back = lax.all_to_all(turned.reshape(8, 40, 256), BAND, 0, 0, tiled=True)
    return back.reshape(4, 2, 40, 256).transpose(2, 0, 1, 3).reshape(40, 4, PLANE)


def solution(mesh):
    fine = Mesh(mesh.devices.reshape(4, 4, 2, 4, 2), SPACE + BAND)
    placed = (P(BAND, SPACE, None), P(SPACE, None), P())
    return jax.shard_map(
        local, mesh=fine, in_specs=placed, out_specs=P(BAND, SPACE, None), check_vma=False
    )
```

```python
import functools

import jax
import jax.numpy as jnp
import numpy as np
from jax import lax
from jax.experimental import pallas as pl
from jax.experimental.pallas import tpu as pltpu
from jax.sharding import Mesh
from jax.sharding import PartitionSpec as P


DEG = 4
NY = 16
NZ = 32
PLANE = NY * NZ
NORB = 320
BAND = ("x", "zl")
SPACE = ("y", "zh", "core")

coef_lap = (-205.0 / 72.0, 8.0 / 5.0, -1.0 / 5.0, 8.0 / 315.0, -1.0 / 560.0)
center_val = 6.0
half_width = 4.0
SCALE = -0.5 / half_width


def lateral():
    def ring(n):
        m = np.zeros((n, n))
        for k in range(1, 5):
            for i in range(n):
                m[i, (i + k) % n] += coef_lap[k]
                m[i, (i - k) % n] += coef_lap[k]
        return m

    lap = np.kron(np.eye(NY), ring(NZ)) + np.kron(ring(NY), np.eye(NZ))
    lap += 3.0 * coef_lap[0] * np.eye(PLANE)
    full = (SCALE * lap - (center_val / half_width) * np.eye(PLANE)).astype(np.float32)
    high = full.astype(jnp.bfloat16)
    low = (full - high.astype(np.float32)).astype(jnp.bfloat16)
    return high, low


def split(v):
    high = v.astype(jnp.bfloat16)
    low = (v - high.astype(jnp.float32)).astype(jnp.bfloat16)
    return high, low


def place(ref, at, buf_ref, pot_ref):
    rows = pl.ds(pl.multiple_of(at, 8), 8)
    for q in range(6):
        for j in range(4):
            part = jnp.concatenate(
                [ref[s, q, :, j * 128 : (j + 1) * 128] for s in range(2)], axis=0
            )
            if q < 5:
                buf_ref[q, j, rows, :] = part
            else:
                pot_ref[j, rows, :] = part * (1.0 / half_width)


def advance(spans, cur, prev, pot_ref, pot_at, mh_ref, ml_ref, part_ref, emit):
    tall = sum(count for _, count in spans) * 5
    twice = 1.0 if prev is None else 2.0
    places = [(q, at, n) for q in range(5) for at, n in spans]
    lanes = []
    for j in range(4):
        parts = [cur[q, j, 4 + at : 4 + at + n, :] for q, at, n in places]
        lanes.append(twice * jnp.concatenate(parts, axis=0))
    high, low = split(jnp.concatenate(lanes, axis=1))
    dot = lambda a, b: jnp.dot(a, b, preferred_element_type=jnp.float32)
    both = dot(jnp.concatenate([high, low], axis=0), mh_ref[...])
    rest = dot(high, ml_ref[...])
    row = 0
    for q, at, n in places:
        for j in range(4):
            acc = pot_ref[j, pot_at + at : pot_at + at + n, :] * lanes[j][row : row + n]
            for k in range(1, 5):
                acc = acc + (twice * SCALE * coef_lap[k]) * (
                    cur[q, j, 4 + at + k : 4 + at + k + n, :]
                    + cur[q, j, 4 + at - k : 4 + at - k + n, :]
                )
            if prev is not None:
                acc = acc - prev[q, j, 8 + at : 8 + at + n, :]
            part_ref[j, row : row + n, :] = acc
        row += n
    row = 0
    for q, at, n in places:
        for j in range(4):
            rows, cols = slice(row, row + n), slice(j * 128, j * 128 + 128)
            lat = both[rows, cols] + (both[tall + row : tall + row + n, cols] + rest[rows, cols])
            emit(q, j, at, n, part_ref[j, rows, :] + lat)
        row += n


def saver(ref):
    def emit(q, j, at, n, acc):
        ref[q, j, at : at + n, :] = acc

    return emit


def inner_kernel(*refs):
    mh_ref, ml_ref, pot_ref = refs[4:7]
    levels, part_ref = refs[7:11], refs[11]
    zh_here = lax.axis_index("zh")
    for ahead in range(4):
        place(refs[ahead], lax.rem(zh_here + (4 - ahead), 4) * 8, levels[0], pot_ref)
    for step in range(1, DEG):
        prev = levels[step - 2] if step > 1 else None
        spans = ((0, 32 - 8 * step),)
        advance(
            spans,
            levels[step - 1],
            prev,
            pot_ref,
            4 * step,
            mh_ref,
            ml_ref,
            part_ref,
            saver(levels[step]),
        )


def side_kernel(late, *refs):
    first, from_one, from_three, mh_ref, ml_ref, own_pot = refs[0:6]
    inner, refs = refs[6:10], refs[10:]
    if late:
        done_ref, refs = refs[0], refs[1:]
    out_ref, pot_ref, part_ref = refs[0:3]
    levels = refs[3:7]
    zh_here = lax.axis_index("zh")
    if late:
        out_ref[...] = done_ref[...]

    def put(ref, ahead):
        zh = lax.rem(zh_here + (4 - ahead), 4)
        place(ref, jnp.where(zh >= 2, (zh - 2) * 8, 48 + zh * 8), levels[0], pot_ref)

    put(first, 2 if late else 0)
    odd = lax.rem(zh_here, 2)

    @pl.when(odd == (1 if late else 0))
    def _():
        put(from_three, 3)

    @pl.when(odd == (0 if late else 1))
    def _():
        put(from_one, 1)

    def emit(q, j, at, n, acc):
        half, tile = divmod(j, 2)
        for plane in range(at, at + n, 4):
            zh, s = divmod(plane // 4, 2)
            row = ((half * 4 + zh) * 2 + s) * 10 + q * 2 + tile
            out_ref[pl.ds(row, 4, stride=160), :] = acc[plane - at : plane - at + 4, :]

    def run(above):
        pot_ref[:, 16:48, :] = own_pot[...]
        for step in range(DEG):
            to, at = (40 - 8 * step, 24 - 8 * step) if above else (16, 0)
            levels[step][:, :, to : to + 8, :] = inner[step][:, :, at : at + 8, :]
        for step in range(1, DEG + 1):
            advance(
                ((48 - 8 * step if above else 0, 16),),
                levels[step - 1],
                levels[step - 2] if step > 1 else None,
                pot_ref,
                4 * step,
                mh_ref,
                ml_ref,
                part_ref,
                emit if step == DEG else saver(levels[step]),
            )

    for above in (False, True):
        pl.when((zh_here < 2) == (above != late))(functools.partial(run, above))


def stack_of(rows):
    return (5, 4, rows, 128)


def run_inner(pieces, lat):
    vmem = pl.BlockSpec(memory_space=pltpu.VMEM)
    shapes = [(4, 32, 128)] + [stack_of(32 - 8 * s) for s in range(DEG)]
    return pl.pallas_call(
        inner_kernel,
        out_shape=[jax.ShapeDtypeStruct(shape, jnp.float32) for shape in shapes],
        in_specs=[vmem] * 6,
        out_specs=[vmem] * 5,
        scratch_shapes=[pltpu.VMEM((4, 120, 128), jnp.float32)],
        compiler_params=pltpu.CompilerParams(vmem_limit_bytes=16 << 20),
        cost_estimate=pl.CostEstimate(flops=2 << 30, bytes_accessed=4 << 20, transcendentals=0),
        name="inner",
    )(*pieces, *lat)


def run_side(late, halos, lat, found, done=()):
    vmem = pl.BlockSpec(memory_space=pltpu.VMEM)
    operands = (*halos, *lat, *found, *done)
    return pl.pallas_call(
        functools.partial(side_kernel, late),
        out_shape=jax.ShapeDtypeStruct((640, 128), jnp.float32),
        in_specs=[vmem] * len(operands),
        out_specs=vmem,
        scratch_shapes=[
            pltpu.VMEM((4, 64, 128), jnp.float32),
            pltpu.VMEM((4, 80, 128), jnp.float32),
        ]
        + [pltpu.VMEM(stack_of(64 - 8 * s), jnp.float32) for s in range(DEG)],
        compiler_params=pltpu.CompilerParams(vmem_limit_bytes=20 << 20),
        cost_estimate=pl.CostEstimate(flops=2 << 30, bytes_accessed=4 << 20, transcendentals=0),
        name="late" if late else "ready",
    )(*operands)


def turn_kernel(weights_ref, high_ref, low_ref):
    high_ref[...], low_ref[...] = split(weights_ref[...].T)


def run_turn(rotation):
    vmem = pl.BlockSpec(memory_space=pltpu.VMEM)
    return pl.pallas_call(
        turn_kernel,
        out_shape=[jax.ShapeDtypeStruct((NORB, NORB), jnp.bfloat16)] * 2,
        in_specs=[vmem],
        out_specs=[vmem] * 2,
        compiler_params=pltpu.CompilerParams(vmem_limit_bytes=8 << 20),
        name="turn",
    )(rotation)


def rotate_kernel(wh_ref, wl_ref, field_ref, out_ref):
    field = jnp.concatenate(
        [field_ref[pl.ds(tile, NORB, stride=2), :] for tile in range(2)], axis=1
    )
    high, low = split(field)
    dot = lambda a, b: jnp.dot(a, b, preferred_element_type=jnp.float32)
    wh = wh_ref[...]
    out_ref[...] = dot(wh, high) + (dot(wh, low) + dot(wl_ref[...], high))


def run_rotate(weights, field):
    vmem = pl.BlockSpec(memory_space=pltpu.VMEM)
    return pl.pallas_call(
        rotate_kernel,
        out_shape=jax.ShapeDtypeStruct((NORB, 256), jnp.float32),
        in_specs=[vmem] * 3,
        out_specs=vmem,
        compiler_params=pltpu.CompilerParams(vmem_limit_bytes=8 << 20),
        name="rotate",
    )(*weights, field)


def finish_kernel(back_ref, out_ref):
    for plane in range(4):
        for tile in range(4):
            half, at = divmod(tile, 2)
            out_ref[pl.ds(tile * 4 + plane, 40, stride=16), :] = back_ref[
                plane * 2 + half, :, at * 128 : at * 128 + 128
            ]


def run_finish(back):
    vmem = pl.BlockSpec(memory_space=pltpu.VMEM)
    return pl.pallas_call(
        finish_kernel,
        out_shape=jax.ShapeDtypeStruct((640, 128), jnp.float32),
        in_specs=[vmem],
        out_specs=vmem,
        compiler_params=pltpu.CompilerParams(vmem_limit_bytes=4 << 20),
        name="finish",
    )(back)


def pack_kernel(keep_ref, pot_ref, got_ref, *out_refs):
    core, zh_here = lax.axis_index("core"), lax.axis_index("zh")
    for ahead in range(4):
        first = lax.rem(zh_here + ahead, 4) * 5
        out_refs[ahead][core, 0:5] = keep_ref[pl.ds(first, 5)]
        out_refs[ahead][core, 5] = pot_ref[...]
        out_refs[ahead][1 - core, 0:5] = got_ref[pl.ds(first, 5)]
        out_refs[ahead][1 - core, 5] = got_ref[20]


def run_pack(keep, pot, got):
    vmem = pl.BlockSpec(memory_space=pltpu.VMEM)
    return pl.pallas_call(
        pack_kernel,
        out_shape=[jax.ShapeDtypeStruct((2, 6, 4, PLANE), jnp.float32)] * 4,
        in_specs=[vmem] * 3,
        out_specs=[vmem] * 4,
        compiler_params=pltpu.CompilerParams(vmem_limit_bytes=4 << 20),
        name="pack",
    )(keep, pot, got)


SWAP = [(0, 1), (1, 0)]


def ahead_by(step):
    return [(zh, (zh + step) % 4) for zh in range(4)]


def outward(ahead):
    pairs = []
    for y in range(4):
        for zh in range(4):
            way = 1 if (zh - ahead) % 4 >= 2 else -1
            pairs.append((y * 4 + zh, (y + way) % 4 * 4 + zh))
    return pairs


def local(orbitals, potential, rotation):
    core = lax.axis_index("core")
    pairs = orbitals.reshape(4, 2, 5, 4, PLANE)
    give = lax.dynamic_index_in_dim(pairs, 1 - core, 1, keepdims=False).reshape(20, 4, PLANE)
    keep = lax.dynamic_index_in_dim(pairs, core, 1, keepdims=False)
    give = jnp.concatenate([give, potential[None]], axis=0)
    got = lax.ppermute(give, "core", SWAP)

    packed = run_pack(keep.reshape(20, 4, PLANE), potential, got)
    pieces, halos = [None] * 4, [None] * 4
    for ahead in (2, 1, 3, 0):
        piece = packed[ahead]
        pieces[ahead] = lax.ppermute(piece, "zh", ahead_by(ahead)) if ahead else piece
    for ahead in (0, 2, 1, 3):
        halos[ahead] = lax.ppermute(pieces[ahead], ("y", "zh"), outward(ahead))
    lat = tuple(jnp.asarray(part) for part in lateral())
    found = run_inner(pieces, lat)
    done = run_side(False, (halos[0], halos[1], halos[3]), lat, found)
    filtered = run_side(True, (halos[2], halos[1], halos[3]), lat, found, (done,))
    weights = run_turn(rotation)
    filtered, weights = lax.optimization_barrier((filtered, weights))
    columns = lax.all_to_all(
        filtered.reshape(64, 5, 2, 128), BAND + ("zh", "core"), 0, 0, tiled=True
    )
    turned = run_rotate(weights, columns.reshape(640, 128))
    back = lax.all_to_all(turned.reshape(8, 40, 256), BAND, 0, 0, tiled=True)
    return run_finish(back).reshape(40, 4, 4, 128).transpose(0, 2, 1, 3).reshape(40, 4, PLANE)


def solution(mesh):
    fine = Mesh(mesh.devices.reshape(4, 4, 2, 4, 2), SPACE + BAND)
    placed = (P(BAND, SPACE, None), P(SPACE, None), P())
    return jax.shard_map(
        local, mesh=fine, in_specs=placed, out_specs=P(BAND, SPACE, None), check_vma=False
    )
```

```python
import functools

import jax
import jax.numpy as jnp
import numpy as np
from jax import lax
from jax.experimental import pallas as pl
from jax.experimental.pallas import tpu as pltpu
from jax.sharding import Mesh
from jax.sharding import PartitionSpec as P


DEG = 4
NY = 16
NZ = 32
PLANE = NY * NZ
NORB = 320
BAND = ("x", "zl")
SPACE = ("y", "zh", "core")

coef_lap = (-205.0 / 72.0, 8.0 / 5.0, -1.0 / 5.0, 8.0 / 315.0, -1.0 / 560.0)
center_val = 6.0
half_width = 4.0
SCALE = -0.5 / half_width


def lateral():
    def ring(n):
        m = np.zeros((n, n))
        for k in range(1, 5):
            for i in range(n):
                m[i, (i + k) % n] += coef_lap[k]
                m[i, (i - k) % n] += coef_lap[k]
        return m

    lap = np.kron(np.eye(NY), ring(NZ)) + np.kron(ring(NY), np.eye(NZ))
    lap += 3.0 * coef_lap[0] * np.eye(PLANE)
    full = (SCALE * lap - (center_val / half_width) * np.eye(PLANE)).astype(np.float32)
    high = full.astype(jnp.bfloat16)
    low = (full - high.astype(np.float32)).astype(jnp.bfloat16)
    return high, low


def split(v):
    high = v.astype(jnp.bfloat16)
    low = (v - high.astype(jnp.float32)).astype(jnp.bfloat16)
    return high, low


def place(ref, at, buf_ref, pot_ref):
    rows = pl.ds(pl.multiple_of(at, 8), 8)
    for q in range(6):
        for j in range(4):
            part = jnp.concatenate(
                [ref[s, q, :, j * 128 : (j + 1) * 128] for s in range(2)], axis=0
            )
            if q < 5:
                buf_ref[q, j, rows, :] = part
            else:
                pot_ref[j, rows, :] = part * (1.0 / half_width)


def advance(spans, cur, prev, pot_ref, pot_at, mh_ref, ml_ref, part_ref, emit):
    tall = sum(count for _, count in spans) * 5
    twice = 1.0 if prev is None else 2.0
    places = [(q, at, n) for q in range(5) for at, n in spans]
    lanes = []
    for j in range(4):
        parts = [cur[q, j, 4 + at : 4 + at + n, :] for q, at, n in places]
        lanes.append(twice * jnp.concatenate(parts, axis=0))
    high, low = split(jnp.concatenate(lanes, axis=1))
    dot = lambda a, b: jnp.dot(a, b, preferred_element_type=jnp.float32)
    both = dot(jnp.concatenate([high, low], axis=0), mh_ref[...])
    rest = dot(high, ml_ref[...])
    row = 0
    for q, at, n in places:
        for j in range(4):
            acc = pot_ref[j, pot_at + at : pot_at + at + n, :] * lanes[j][row : row + n]
            for k in range(1, 5):
                acc = acc + (twice * SCALE * coef_lap[k]) * (
                    cur[q, j, 4 + at + k : 4 + at + k + n, :]
                    + cur[q, j, 4 + at - k : 4 + at - k + n, :]
                )
            if prev is not None:
                acc = acc - prev[q, j, 8 + at : 8 + at + n, :]
            part_ref[j, row : row + n, :] = acc
        row += n
    row = 0
    for q, at, n in places:
        for j in range(4):
            rows, cols = slice(row, row + n), slice(j * 128, j * 128 + 128)
            lat = both[rows, cols] + (both[tall + row : tall + row + n, cols] + rest[rows, cols])
            emit(q, j, at, n, part_ref[j, rows, :] + lat)
        row += n


def saver(ref):
    def emit(q, j, at, n, acc):
        ref[q, j, at : at + n, :] = acc

    return emit


def inner_kernel(*refs):
    mh_ref, ml_ref, pot_ref = refs[4:7]
    levels, part_ref = refs[7:11], refs[11]
    zh_here = lax.axis_index("zh")
    for ahead in range(4):
        place(refs[ahead], lax.rem(zh_here + (4 - ahead), 4) * 8, levels[0], pot_ref)
    for step in range(1, DEG):
        prev = levels[step - 2] if step > 1 else None
        spans = ((0, 32 - 8 * step),)
        advance(
            spans,
            levels[step - 1],
            prev,
            pot_ref,
            4 * step,
            mh_ref,
            ml_ref,
            part_ref,
            saver(levels[step]),
        )


def side_kernel(late, *refs):
    first, from_one, from_three, mh_ref, ml_ref, own_pot = refs[0:6]
    inner, refs = refs[6:10], refs[10:]
    if late:
        done_ref, refs = refs[0], refs[1:]
    out_ref, pot_ref, part_ref = refs[0:3]
    levels = refs[3:7]
    zh_here = lax.axis_index("zh")
    if late:
        out_ref[...] = done_ref[...]

    def put(ref, ahead):
        zh = lax.rem(zh_here + (4 - ahead), 4)
        place(ref, jnp.where(zh >= 2, (zh - 2) * 8, 48 + zh * 8), levels[0], pot_ref)

    put(first, 2 if late else 0)
    odd = lax.rem(zh_here, 2)

    @pl.when(odd == (1 if late else 0))
    def _():
        put(from_three, 3)

    @pl.when(odd == (0 if late else 1))
    def _():
        put(from_one, 1)

    def emit(q, j, at, n, acc):
        half, tile = divmod(j, 2)
        for plane in range(at, at + n, 4):
            zh, s = divmod(plane // 4, 2)
            row = ((half * 4 + zh) * 2 + s) * 10 + q * 2 + tile
            out_ref[pl.ds(row, 4, stride=160), :] = acc[plane - at : plane - at + 4, :]

    def run(above):
        pot_ref[:, 16:48, :] = own_pot[...]
        for step in range(DEG):
            to, at = (40 - 8 * step, 24 - 8 * step) if above else (16, 0)
            levels[step][:, :, to : to + 8, :] = inner[step][:, :, at : at + 8, :]
        for step in range(1, DEG + 1):
            advance(
                ((48 - 8 * step if above else 0, 16),),
                levels[step - 1],
                levels[step - 2] if step > 1 else None,
                pot_ref,
                4 * step,
                mh_ref,
                ml_ref,
                part_ref,
                emit if step == DEG else saver(levels[step]),
            )

    for above in (False, True):
        pl.when((zh_here < 2) == (above != late))(functools.partial(run, above))


def stack_of(rows):
    return (5, 4, rows, 128)


def run_inner(pieces, lat):
    vmem = pl.BlockSpec(memory_space=pltpu.VMEM)
    shapes = [(4, 32, 128)] + [stack_of(32 - 8 * s) for s in range(DEG)]
    return pl.pallas_call(
        inner_kernel,
        out_shape=[jax.ShapeDtypeStruct(shape, jnp.float32) for shape in shapes],
        in_specs=[vmem] * 6,
        out_specs=[vmem] * 5,
        scratch_shapes=[pltpu.VMEM((4, 120, 128), jnp.float32)],
        compiler_params=pltpu.CompilerParams(vmem_limit_bytes=16 << 20),
        cost_estimate=pl.CostEstimate(flops=2 << 30, bytes_accessed=4 << 20, transcendentals=0),
        name="inner",
    )(*pieces, *lat)


def run_side(late, halos, lat, found, done=()):
    vmem = pl.BlockSpec(memory_space=pltpu.VMEM)
    operands = (*halos, *lat, *found, *done)
    return pl.pallas_call(
        functools.partial(side_kernel, late),
        out_shape=jax.ShapeDtypeStruct((640, 128), jnp.float32),
        in_specs=[vmem] * len(operands),
        out_specs=vmem,
        scratch_shapes=[
            pltpu.VMEM((4, 64, 128), jnp.float32),
            pltpu.VMEM((4, 80, 128), jnp.float32),
        ]
        + [pltpu.VMEM(stack_of(64 - 8 * s), jnp.float32) for s in range(DEG)],
        compiler_params=pltpu.CompilerParams(vmem_limit_bytes=20 << 20),
        cost_estimate=pl.CostEstimate(flops=2 << 30, bytes_accessed=4 << 20, transcendentals=0),
        name="late" if late else "ready",
    )(*operands)


def turn_kernel(weights_ref, high_ref, low_ref):
    high_ref[...], low_ref[...] = split(weights_ref[...].T)


def run_turn(rotation):
    vmem = pl.BlockSpec(memory_space=pltpu.VMEM)
    return pl.pallas_call(
        turn_kernel,
        out_shape=[jax.ShapeDtypeStruct((NORB, NORB), jnp.bfloat16)] * 2,
        in_specs=[vmem],
        out_specs=[vmem] * 2,
        compiler_params=pltpu.CompilerParams(vmem_limit_bytes=8 << 20),
        name="turn",
    )(rotation)


def rotate_kernel(wh_ref, wl_ref, field_ref, out_ref):
    field = jnp.concatenate(
        [field_ref[pl.ds(tile, NORB, stride=2), :] for tile in range(2)], axis=1
    )
    high, low = split(field)
    dot = lambda a, b: jnp.dot(a, b, preferred_element_type=jnp.float32)
    wh = wh_ref[...]
    both = dot(jnp.concatenate([wh, wl_ref[...]], axis=0), high)
    out_ref[...] = both[:NORB] + (both[NORB:] + dot(wh, low))


def run_rotate(weights, field):
    vmem = pl.BlockSpec(memory_space=pltpu.VMEM)
    return pl.pallas_call(
        rotate_kernel,
        out_shape=jax.ShapeDtypeStruct((NORB, 256), jnp.float32),
        in_specs=[vmem] * 3,
        out_specs=vmem,
        compiler_params=pltpu.CompilerParams(vmem_limit_bytes=8 << 20),
        name="rotate",
    )(*weights, field)


def finish_kernel(back_ref, out_ref):
    for plane in range(4):
        for tile in range(4):
            half, at = divmod(tile, 2)
            out_ref[pl.ds(tile * 4 + plane, 40, stride=16), :] = back_ref[
                plane * 2 + half, :, at * 128 : at * 128 + 128
            ]


def run_finish(back):
    vmem = pl.BlockSpec(memory_space=pltpu.VMEM)
    return pl.pallas_call(
        finish_kernel,
        out_shape=jax.ShapeDtypeStruct((640, 128), jnp.float32),
        in_specs=[vmem],
        out_specs=vmem,
        compiler_params=pltpu.CompilerParams(vmem_limit_bytes=4 << 20),
        name="finish",
    )(back)


SWAP = [(0, 1), (1, 0)]


def ahead_by(step):
    return [(zh, (zh + step) % 4) for zh in range(4)]


def outward(ahead):
    pairs = []
    for y in range(4):
        for zh in range(4):
            way = 1 if (zh - ahead) % 4 >= 2 else -1
            pairs.append((y * 4 + zh, (y + way) % 4 * 4 + zh))
    return pairs


def local(orbitals, potential, rotation):
    core, zh_here = lax.axis_index("core"), lax.axis_index("zh")
    pairs = orbitals.reshape(4, 2, 5, 4, PLANE)
    give = lax.dynamic_index_in_dim(pairs, 1 - core, 1, keepdims=False).reshape(20, 4, PLANE)
    keep = lax.dynamic_index_in_dim(pairs, core, 1, keepdims=False)
    give = jnp.concatenate([give, potential[None]], axis=0)
    got = lax.ppermute(give, "core", SWAP)

    def six(block, pot):
        block = block.reshape(4, 5, 4, PLANE)
        return jnp.concatenate(
            [block, jnp.broadcast_to(pot[None, None], (4, 1, 4, PLANE))], axis=1
        )

    own = six(keep, potential)
    other = six(got[:20], got[20])
    payload = jnp.where(
        core == 0,
        jnp.stack([own, other], axis=1),
        jnp.stack([other, own], axis=1),
    )
    pieces, halos = [None] * 4, [None] * 4
    for ahead in (2, 1, 3, 0):
        piece = lax.dynamic_index_in_dim(payload, (zh_here + ahead) % 4, 0, keepdims=False)
        pieces[ahead] = lax.ppermute(piece, "zh", ahead_by(ahead)) if ahead else piece
    for ahead in (0, 2, 1, 3):
        halos[ahead] = lax.ppermute(pieces[ahead], ("y", "zh"), outward(ahead))
    lat = tuple(jnp.asarray(part) for part in lateral())
    found = run_inner(pieces, lat)
    done = run_side(False, (halos[0], halos[1], halos[3]), lat, found)
    filtered = run_side(True, (halos[2], halos[1], halos[3]), lat, found, (done,))
    weights = run_turn(rotation)
    filtered, weights = lax.optimization_barrier((filtered, weights))
    columns = lax.all_to_all(
        filtered.reshape(64, 5, 2, 128), BAND + ("zh", "core"), 0, 0, tiled=True
    )
    turned = run_rotate(weights, columns.reshape(640, 128))
    back = lax.all_to_all(turned.reshape(8, 40, 256), BAND, 0, 0, tiled=True)
    return run_finish(back).reshape(40, 4, 4, 128).transpose(0, 2, 1, 3).reshape(40, 4, PLANE)


def solution(mesh):
    fine = Mesh(mesh.devices.reshape(4, 4, 2, 4, 2), SPACE + BAND)
    placed = (P(BAND, SPACE, None), P(SPACE, None), P())
    return jax.shard_map(
        local, mesh=fine, in_specs=placed, out_specs=P(BAND, SPACE, None), check_vma=False
    )
```
